256 devices in a mesh: row: 16 (over z, core), col: 16 (over x, y).
Axes of the slice: x: 4, y: 4, z: 8, core: 2. Of those that a mesh axis runs over, the one named last changes fastest.
Arguments:
- tiles: float32 [16, 16, 16, 128, 128], P('row', 'col'), may hold values from -1 to 1
- tile_rows: int32 [16, 16, 16], P('row', 'col'), may hold values from 0 to 63, as said below
- tile_cols: int32 [16, 16, 16], P('row', 'col'), may hold values from 0 to 63
- tile_counts: int32 [16, 16], P('row', 'col'), may hold values from 2 to 16, as said below
- objective: float32 [131072], P('col'), may hold values from -6 to 6
- upper: float32 [131072], P('col'), may hold values from 0.2 to 2
- bound_codes: int32 [131072], P('col'), may hold values from 0 to 2
- rhs: float32 [131072], P('row'), may hold values from -6 to 6
- row_codes: int32 [131072], P('row'), may hold values from 0 to 1
Outputs:
- primal: float32 [131072], P('col')
- dual: float32 [131072], P('row')
The draws below stay inside these ranges and needn't reach their ends.
Inputs may be any that keep to these rules, and one draw needn't show every extreme that they name: `tile_rows`: one device's live slots hold distinct (tile row, tile column) pairs. `tile_counts`: slots at or past a device's count are not part of K; some device has all 16 slots live.
All inputs are finite; a program needn't handle non-finite values. Where the reference program divides by a largest or mean magnitude, that divisor is 1e-20 or more.
Results may differ from the reference program's by a relative error of at most 0.00018.
Values sent between devices are 32-bit elements; how exact they have to be, the bound alone decides.
A program may use at most 64 MiB of HBM per device.

```python
import math
import jax
import jax.numpy as jnp
from jax import lax

TILE = 128
TILES_DEV = 16
TILE_ROWS = 64
TILE_COLS = 64
OUTER = 2
INNER = 4
ROWS = 131072
COLUMNS = 131072
N_ROW = 16
N_COL = 16


def tile_slots(key):
    device_keys = jax.random.split(jax.random.fold_in(key, 11), N_ROW * N_COL)
    chosen = jax.vmap(lambda single: jax.random.permutation(single, TILE_ROWS * TILE_COLS)[:TILES_DEV])(device_keys)
    return chosen.reshape(N_ROW, N_COL, TILES_DEV).astype(jnp.int32)


def draw_tile_rows(key, part):
    return (tile_slots(key) // TILE_COLS).astype(jnp.int32)


def draw_tile_cols(key, part):
    return (tile_slots(key) % TILE_COLS).astype(jnp.int32)


def draw_tile_counts(key, part):
    first_key, second_key = jax.random.split(jax.random.fold_in(key, 23))
    halvings = jax.random.randint(first_key, (N_ROW, N_COL), 0, 4).astype(jnp.int32)
    counts = jnp.right_shift(jnp.full((N_ROW, N_COL), TILES_DEV, jnp.int32), halvings)
    fullest = jax.random.randint(second_key, (), 0, N_ROW * N_COL).astype(jnp.int32)
    positions = jnp.arange(N_ROW * N_COL, dtype=jnp.int32).reshape(N_ROW, N_COL)
    return jnp.where(positions == fullest, TILES_DEV, counts).astype(jnp.int32)


def draw_tiles(key, part):
    full_shape = (N_ROW, N_COL, TILES_DEV, TILE, TILE)
    entry_key, row_key = jax.random.split(jax.random.fold_in(key, 37), 2)
    entries = jnp.clip(jax.random.normal(entry_key, full_shape, jnp.float32), -6.0, 6.0)
    row_scale = jnp.exp(jax.random.uniform(row_key, (N_ROW, N_COL, TILES_DEV, TILE, 1), jnp.float32, -1.2, 1.2))
    spread_size = max(N_COL * TILES_DEV * TILE // (2 * TILE_ROWS), 1)
    return jnp.clip(entries * row_scale / math.sqrt(spread_size), -1.0, 1.0).astype(jnp.float32)


def touch_ends(array, rng, least, high):
    longest = array.shape.index(max(array.shape))
    spots = []
    for shift in (0, 1):
        where = [jax.random.randint(jax.random.fold_in(rng, axis), (), 0, length) for axis, length in enumerate(array.shape)]
        where[longest] = (where[longest] + shift) % array.shape[longest]
        spots.append(tuple(where))
    return array.at[spots[0]].set(least).at[spots[1]].set(high)


def levels(own_key, dims, cuts, smallest, high):
    def one(position, parts):
        heights = jax.random.uniform(jax.random.fold_in(jax.random.fold_in(own_key, 6), position), (parts,), jnp.float32, smallest / len(cuts), high / len(cuts))
        return jnp.repeat(jnp.exp(heights), dims[position] // parts).reshape((-1,) + (1,) * (len(dims) - position - 1))

    factor_of = one(*cuts[0])
    for cut in cuts[1:]:
        factor_of = factor_of * one(*cut)
    return factor_of


def gaussian(own_key, dims, spread, bound, shards=(), held_as=jnp.bfloat16):
    level = levels(own_key, dims, shards, -0.22, 0.18) if shards else 1.0
    values = jax.random.normal(own_key, dims, jnp.float32) * spread * level
    return jnp.minimum(jnp.maximum(values, -bound), bound).astype(held_as)


def setup_inputs(seed: int = 0) -> dict:
    splits = jax.random.split(jax.random.key(seed), 10)
    return {
        "tiles": draw_tiles(jax.random.fold_in(splits[9], 71), 0),
        "tile_rows": draw_tile_rows(jax.random.fold_in(splits[9], 71), 0),
        "tile_cols": draw_tile_cols(jax.random.fold_in(splits[9], 71), 0),
        "tile_counts": draw_tile_counts(jax.random.fold_in(splits[9], 71), 0),
        "objective": gaussian(splits[4], (COLUMNS,), 1.0, 6.0, ((0, 16),), jnp.float32),
        "upper": jnp.clip(jnp.exp(math.log(2.0) - 2.3025851 * jax.random.uniform(splits[5], (COLUMNS,), jnp.float32) ** levels(splits[5], (COLUMNS,), ((0, 16),), -0.2, 0.2)), 0.2, 2.0),
        "bound_codes": touch_ends(jax.random.randint(splits[6], (COLUMNS,), 0, 3), jax.random.fold_in(splits[6], 1), 0, 2).astype(jnp.int32),
        "rhs": gaussian(splits[7], (ROWS,), 1.0, 6.0, ((0, 16),), jnp.float32),
        "row_codes": touch_ends(jax.random.randint(splits[8], (ROWS,), 0, 2), jax.random.fold_in(splits[8], 1), 0, 1).astype(jnp.int32),
    }


def project_primal(values, bound_codes, upper):
    values = jnp.where(bound_codes >= 1, jnp.maximum(values, 0.0), values)
    return jnp.where(bound_codes == 2, jnp.minimum(values, upper), values)

def project_dual(values, row_codes):
    return jnp.where(row_codes == 1, jnp.maximum(values, 0.0), values)

def step_update(step_size, weight, inter_term, primal_sq, dual_sq, counter):
    shrink = 1.0 - (counter + 1) ** (-0.3)
    growth = 1.0 + (counter + 1) ** (-0.6)
    numer = shrink * (weight * primal_sq + dual_sq / weight + 1e-06)
    return numer / jnp.maximum(2.0 * jnp.abs(inter_term), numer / (growth * step_size))

def reference(tiles, tile_rows, tile_cols, tile_counts, objective, upper, bound_codes, rhs, row_codes):
    highest = lax.Precision.HIGHEST
    slots = jnp.arange(TILES_DEV, dtype=jnp.int32)
    alive = (slots[None, None, :] < tile_counts[:, :, None]).astype(jnp.float32)
    row_hot = (tile_rows[..., None] == jnp.arange(TILE_ROWS, dtype=jnp.int32)).astype(jnp.float32)
    col_hot = (tile_cols[..., None] == jnp.arange(TILE_COLS, dtype=jnp.int32)).astype(jnp.float32)
    row_live = row_hot * alive[..., None]
    col_live = col_hot * alive[..., None]

    def forward(vector):
        shaped = vector.reshape(N_COL, TILE_COLS, TILE)
        pieces = jnp.einsum('rctk,ckj->rctj', col_hot, shaped, precision=highest)
        images = jnp.einsum('rctij,rctj->rcti', tiles, pieces, precision=highest)
        return jnp.einsum('rctk,rcti->rki', row_live, images, precision=highest).reshape(-1)

    def backward(vector):
        shaped = vector.reshape(N_ROW, TILE_ROWS, TILE)
        pieces = jnp.einsum('rctk,rki->rcti', row_hot, shaped, precision=highest)
        images = jnp.einsum('rctij,rcti->rctj', tiles, pieces, precision=highest)
        return jnp.einsum('rctk,rctj->ckj', col_live, images, precision=highest).reshape(-1)
    largest = jnp.max(jnp.abs(tiles) * alive[:, :, :, None, None])
    step_size = 0.05 / (largest + 1e-06)
    weight = jnp.sqrt((jnp.sum(objective * objective) + 1e-06) / (jnp.sum(rhs * rhs) + 1e-06))
    primal = jnp.zeros_like(objective)
    dual = jnp.zeros_like(rhs)
    row_image = jnp.zeros_like(rhs)
    col_image = jnp.zeros_like(objective)
    counter = 0
    for cycle_index in range(OUTER):
        start_primal = primal
        start_dual = dual
        primal_total = jnp.zeros_like(objective)
        dual_total = jnp.zeros_like(rhs)
        weight_total = jnp.zeros((), jnp.float32)
        for step_index in range(INNER):
            counter += 1
            next_primal = project_primal(primal - step_size / weight * (objective - col_image), bound_codes, upper)
            next_row = forward(next_primal)
            next_dual = project_dual(dual + step_size * weight * (rhs - (2.0 * next_row - row_image)), row_codes)
            next_col = backward(next_dual)
            primal_move = next_primal - primal
            dual_move = next_dual - dual
            inter_term = jnp.sum(primal_move * (next_col - col_image))
            primal_sq = jnp.sum(primal_move * primal_move)
            dual_sq = jnp.sum(dual_move * dual_move)
            primal_total = primal_total + step_size * next_primal
            dual_total = dual_total + step_size * next_dual
            weight_total = weight_total + step_size
            step_size = step_update(step_size, weight, inter_term, primal_sq, dual_sq, counter)
            primal, dual, row_image, col_image = (next_primal, next_dual, next_row, next_col)
        primal = primal_total / weight_total
        dual = dual_total / weight_total
        primal_drift = jnp.sum((primal - start_primal) * (primal - start_primal))
        dual_drift = jnp.sum((dual - start_dual) * (dual - start_dual))
        weight = jnp.sqrt(weight * jnp.sqrt(dual_drift + 1e-06) / jnp.sqrt(primal_drift + 1e-06))
        row_image = forward(primal)
        col_image = backward(dual)
    return (primal, dual)
```

```python
import functools

import jax
import jax.numpy as jnp
from jax import lax
from jax.experimental import pallas as pl
from jax.experimental.pallas import tpu as pltpu
from jax.sharding import PartitionSpec as P

MESH = pl.DeviceIdType.MESH
TILE = 128
SLOTS = 16
GRID = 64
FULL = GRID + SLOTS
OUTER = 2
INNER = 4
STEPS = OUTER * INNER
GROUP = 16
MSG = SLOTS + 8
PAIRS = SLOTS // 2
F32 = jnp.float32
BF16 = jnp.bfloat16


def split3(x):
    hi = x.astype(BF16)
    rest = x - hi.astype(F32)
    mid = rest.astype(BF16)
    lo = (rest - mid.astype(F32)).astype(BF16)
    return hi, mid, lo


def total(x):
    return jnp.sum(jnp.sum(x, axis=0, keepdims=True), axis=1, keepdims=True)


def lane_sums(x):
    return jnp.sum(x, axis=0, keepdims=True)


def col_peers(row, col):
    x, y = col // 4, col % 4
    offsets = [(dx, dy) for dx in range(4) for dy in range(4) if dx or dy]
    offsets.sort(key=lambda o: -(min(o[0], 4 - o[0]) + min(o[1], 4 - o[1])))
    return [(row, ((x + dx) % 4) * 4 + (y + dy) % 4) for dx, dy in offsets]


def row_peers(row, col):
    z, core = row // 2, row % 2
    offsets = [(dz, dc) for dz in range(8) for dc in range(2) if dz or dc]
    offsets.sort(key=lambda o: -(min(o[0], 8 - o[0]) * 2 + o[1]))
    return [(((z + dz) % 8) * 2 + (core + dc) % 2, col) for dz, dc in offsets]


def kernel(
    tiles_hbm, slot_rows, slot_cols, counts, objective, upper, bound_codes, rhs, row_codes,
    primal_out, dual_out,
    tiles, w_forward, w_backward, sum_forward, sum_backward,
    obj, lower, higher, right, floor,
    s_primal, s_dual, s_rows, s_cols, t_primal, t_dual, t_rows, t_cols, b_primal, b_dual,
    scalars, col_buf, row_buf, col_start, row_start,
    tile_sem, col_send, col_recv, row_send, row_recv, start_sem,
):
    row, col = lax.axis_index("row"), lax.axis_index("col")
    live = counts[0]
    fetch = pltpu.make_async_copy(tiles_hbm, tiles, tile_sem)
    fetch.start()

    by_col, by_row = col_peers(row, col), row_peers(row, col)
    barrier = pltpu.get_barrier_semaphore()
    for peer in by_col + by_row:
        pl.semaphore_signal(barrier, inc=1, device_id=peer, device_id_type=MESH)

    def exchange(slots, me, peers, send, recv):
        mine = slots.at[me]
        for peer in peers:
            pltpu.make_async_remote_copy(
                src_ref=mine, dst_ref=mine, send_sem=send, recv_sem=recv,
                device_id=peer, device_id_type=MESH,
            ).start()

    def arrive(slots, send, recv):
        others = slots.at[pl.ds(0, GROUP - 1)]
        pltpu.make_async_copy(others, others, recv).wait()
        pltpu.make_async_copy(others, others, send).wait()

    def widen(dst, src, indices):
        dst[0:GRID, :] = src[...]
        for t in range(SLOTS):
            dst[GRID + t : GRID + t + 1, :] = src[pl.ds(indices[t], 1), :]

    widen(obj, objective, slot_cols)
    widen(right, rhs, slot_rows)
    infinity = jnp.inf
    lower[0:GRID, :] = jnp.where(bound_codes[...] >= 1, 0.0, -infinity)
    higher[0:GRID, :] = jnp.where(bound_codes[...] == 2, upper[...], infinity)
    floor[0:GRID, :] = jnp.where(row_codes[...] == 1, 0.0, -infinity)
    for t in range(SLOTS):
        at = slice(GRID + t, GRID + t + 1)
        code = bound_codes[pl.ds(slot_cols[t], 1), :]
        lower[at, :] = jnp.where(code >= 1, 0.0, -infinity)
        higher[at, :] = jnp.where(code == 2, upper[pl.ds(slot_cols[t], 1), :], infinity)
        floor[at, :] = jnp.where(row_codes[pl.ds(slot_rows[t], 1), :] == 1, 0.0, -infinity)

    rows8 = lax.broadcasted_iota(jnp.int32, (8, TILE), 0)
    lanes8 = lax.broadcasted_iota(jnp.int32, (8, TILE), 1)
    entry = rows8 * TILE + lanes8

    def index_tile(indices, me):
        placed = jnp.zeros((8, TILE), F32)
        for t in range(SLOTS):
            placed = jnp.where(entry == me * SLOTS + t, indices[t].astype(F32), placed)
        return placed

    def slot_column(indices):
        column = jnp.zeros((SLOTS, 2 * TILE), F32)
        which = lax.broadcasted_iota(jnp.int32, (SLOTS, 2 * TILE), 0)
        for t in range(SLOTS):
            column = jnp.where(which == t, indices[t].astype(F32), column)
        return column

    def sum_matrix(dst, summed, indices):
        entries = jnp.concatenate([summed[0:1, :], summed[1:2, :]], axis=1)
        block = lax.broadcasted_iota(jnp.int32, (GRID, 2 * TILE), 0).astype(F32)
        dst[0:GRID, :] = jnp.where(block == entries, 1.0, 0.0).astype(BF16)
        dst[GRID:FULL, :] = jnp.where(slot_column(indices) == entries, 1.0, 0.0).astype(BF16)

    fetch.wait()
    largest = jnp.zeros((8, TILE), F32)
    for t in range(SLOTS):
        tile = jnp.where(t < live, tiles[t], 0.0)
        tiles[t] = tile
        largest = jnp.maximum(largest, jnp.max(jnp.abs(tile).reshape(16, 8, TILE), axis=0))

    row_start[row] = jnp.where(
        rows8 < 2,
        index_tile(slot_cols, row),
        jnp.where(
            rows8 == 2,
            jnp.max(largest, axis=0, keepdims=True),
            jnp.where(rows8 == 3, lane_sums(rhs[...] * rhs[...]), 0.0),
        ),
    )
    pl.semaphore_wait(barrier, 2 * (GROUP - 1))
    exchange(row_start, row, by_row, start_sem.at[0], start_sem.at[1])

    for t in range(SLOTS):
        tile = tiles[t]
        at = slice(TILE * (t % 2), TILE * (t % 2) + TILE)
        for weights, block in ((w_backward, tile), (w_forward, tile.T)):
            hi = block.astype(BF16)
            weights[t // 2, 0:TILE, at] = hi
            weights[t // 2, TILE : 2 * TILE, at] = (block - hi.astype(F32)).astype(BF16)
    for state in (s_primal, s_dual, s_rows, s_cols, t_primal, t_dual, t_rows, t_cols, b_primal, b_dual):
        state[...] = jnp.zeros_like(state)

    arrive(row_start, start_sem.at[0], start_sem.at[1])
    got = row_start[...]
    summed = jnp.sum(got, axis=0)
    most = jnp.max(jnp.max(got, axis=0)[2:3, :], axis=1, keepdims=True)
    right_sq = jnp.sum(summed[3:4, :], axis=1, keepdims=True)
    col_start[col] = jnp.where(
        rows8 < 2,
        index_tile(slot_rows, col),
        jnp.where(
            rows8 == 2, most, jnp.where(rows8 == 3, lane_sums(objective[...] * objective[...]), 0.0)
        ),
    )
    exchange(col_start, col, by_col, start_sem.at[2], start_sem.at[3])
    sum_matrix(sum_backward, summed, slot_cols)
    arrive(col_start, start_sem.at[2], start_sem.at[3])
    got = col_start[...]
    summed = jnp.sum(got, axis=0)
    sum_matrix(sum_forward, summed, slot_rows)
    most = jnp.max(jnp.max(got, axis=0)[2:3, :], axis=1, keepdims=True)
    object_sq = jnp.sum(summed[3:4, :], axis=1, keepdims=True)
    ones = jnp.ones((1, TILE), F32)
    scalars[0:1, :] = 0.05 / (most + 1e-06) * ones
    scalars[1:2, :] = jnp.sqrt((object_sq + 1e-06) / (right_sq + 1e-06)) * ones
    scalars[2:3, :] = jnp.zeros((1, TILE), F32)

    def images(weights, pieces):
        stacked = jnp.concatenate(split3(pieces), axis=0)
        operand = jnp.concatenate([stacked, stacked], axis=1)
        which = lax.broadcasted_iota(jnp.int32, (8, TILE), 0)
        halves = [jnp.zeros((8, TILE), F32), jnp.zeros((8, TILE), F32)]
        for pair in range(PAIRS):
            product = jnp.dot(operand, weights[pair], preferred_element_type=F32)
            half, first = pair // 4, 2 * pair % 8
            base = 8 * half
            both = sum(product[base + SLOTS * s : base + SLOTS * s + 8, :] for s in range(3))
            halves[half] = jnp.where(which == first, both[:, 0:TILE], halves[half])
            halves[half] = jnp.where(which == first + 1, both[:, TILE : 2 * TILE], halves[half])
        return halves

    def summed_rows(matrix, slots):
        data = slots[:, 0:SLOTS, :].reshape(GROUP * SLOTS, TILE)
        ones_at = matrix[...]
        return sum(jnp.dot(ones_at, part, preferred_element_type=F32) for part in split3(data))

    def post(slots, me, halves, sums):
        slots[me, 0:8, :] = halves[0]
        slots[me, 8:SLOTS, :] = halves[1]
        tile = jnp.zeros((8, TILE), F32)
        for i, value in enumerate(sums):
            tile = jnp.where(rows8 == i, value, tile)
        slots[me, SLOTS:MSG, :] = tile

    def gathered_sums(slots, number):
        tiles_in = jnp.sum(slots[:, SLOTS:MSG, :], axis=0)
        lanes = jnp.sum(tiles_in, axis=1, keepdims=True)
        return [lanes[i : i + 1, :] for i in range(number)]

    def iteration(k, _):
        parity = lax.rem(k, 2)
        last = k == STEPS - 1
        restart = k == INNER - 1
        step, weight = scalars[0:1, :], scalars[1:2, :]
        weight_total = scalars[2:3, :] + step
        primal = s_primal[...]
        next_primal = jnp.minimum(
            jnp.maximum(primal - step / weight * (obj[...] - s_cols[...]), lower[...]), higher[...]
        )
        halves = images(w_forward, next_primal[GRID:FULL, :])
        total_primal = t_primal[...] + step * next_primal
        mean_primal = total_primal / weight_total
        move = (next_primal - primal)[0:GRID, :]
        drift = (mean_primal - b_primal[...])[0:GRID, :]
        slots = col_buf.at[parity]
        post(slots, col, halves, (lane_sums(move * move), lane_sums(drift * drift)))
        exchange(slots, col, by_col, col_send, col_recv.at[parity])
        s_primal[...] = jnp.where(restart, mean_primal, next_primal)
        t_primal[...] = jnp.where(restart, 0.0, total_primal)
        b_primal[...] = jnp.where(restart, mean_primal, b_primal[...])

        @pl.when(last)
        def _():
            primal_out[...] = mean_primal[0:GRID, :]

        arrive(slots, col_send, col_recv.at[parity])
        next_rows = summed_rows(sum_forward, slots)
        primal_sq, primal_drift = gathered_sums(slots, 2)
        rows = s_rows[...]
        dual = s_dual[...]
        next_dual = jnp.maximum(
            dual + step * weight * (right[...] - (2.0 * next_rows - rows)), floor[...]
        )
        total_dual = t_dual[...] + step * next_dual
        mean_dual = total_dual / weight_total

        @pl.when(last)
        def _():
            dual_out[...] = mean_dual[0:GRID, :]

        @pl.when(jnp.logical_not(last))
        def _():
            halves = images(w_backward, next_dual[GRID:FULL, :])
            move = (next_dual - dual)[0:GRID, :]
            image_move = (next_rows - rows)[0:GRID, :]
            drift = (mean_dual - b_dual[...])[0:GRID, :]
            slots = row_buf.at[parity]
            post(
                slots, row, halves,
                (lane_sums(move * move), lane_sums(move * image_move), lane_sums(drift * drift)),
            )
            exchange(slots, row, by_row, row_send, row_recv.at[parity])
            total_rows = t_rows[...] + step * next_rows
            s_dual[...] = jnp.where(restart, mean_dual, next_dual)
            t_dual[...] = jnp.where(restart, 0.0, total_dual)
            b_dual[...] = jnp.where(restart, mean_dual, b_dual[...])
            s_rows[...] = jnp.where(restart, total_rows / weight_total, next_rows)
            t_rows[...] = jnp.where(restart, 0.0, total_rows)

            shrink, growth = jnp.float32(0.0), jnp.float32(0.0)
            for i in range(STEPS - 1):
                shrink = jnp.where(k == i, jnp.float32(1.0 - (i + 2) ** (-0.3)), shrink)
                growth = jnp.where(k == i, jnp.float32(1.0 + (i + 2) ** (-0.6)), growth)

            arrive(slots, row_send, row_recv.at[parity])
            next_cols = summed_rows(sum_backward, slots)
            dual_sq, inter, dual_drift = gathered_sums(slots, 3)
            numer = shrink * (weight * primal_sq + dual_sq / weight + 1e-06)
            new_step = numer / jnp.maximum(2.0 * jnp.abs(inter), numer / (growth * step))
            new_weight = jnp.sqrt(
                weight * jnp.sqrt(dual_drift + 1e-06) / jnp.sqrt(primal_drift + 1e-06)
            )
            total_cols = t_cols[...] + step * next_cols
            s_cols[...] = jnp.where(restart, total_cols / weight_total, next_cols)
            t_cols[...] = jnp.where(restart, 0.0, total_cols)
            scalars[0:1, :] = new_step
            scalars[1:2, :] = jnp.where(restart, new_weight, weight)
            scalars[2:3, :] = jnp.where(restart, 0.0, weight_total)

        return 0

    lax.fori_loop(0, STEPS, iteration, 0)


def per_device(
    tiles, tile_rows, tile_cols, tile_counts, objective, upper, bound_codes, rhs, row_codes
):
    vector = lambda: pltpu.VMEM((FULL, TILE), F32)
    blocked = lambda v: v.reshape(GRID, TILE)
    smem = pl.BlockSpec(memory_space=pltpu.SMEM)
    vmem = pl.BlockSpec(memory_space=pltpu.VMEM)
    primal, dual = pl.pallas_call(
        kernel,
        out_shape=(jax.ShapeDtypeStruct((GRID, TILE), F32),) * 2,
        in_specs=[pl.BlockSpec(memory_space=pl.ANY), smem, smem, smem] + [vmem] * 5,
        out_specs=(vmem, vmem),
        scratch_shapes=[
            pltpu.VMEM((SLOTS, TILE, TILE), F32),
            pltpu.VMEM((PAIRS, 2 * TILE, 2 * TILE), BF16),
            pltpu.VMEM((PAIRS, 2 * TILE, 2 * TILE), BF16),
            pltpu.VMEM((FULL, 2 * TILE), BF16),
            pltpu.VMEM((FULL, 2 * TILE), BF16),
        ]
        + [vector() for _ in range(15)]
        + [
            pltpu.VMEM((8, TILE), F32),
            pltpu.VMEM((2, GROUP, MSG, TILE), F32),
            pltpu.VMEM((2, GROUP, MSG, TILE), F32),
            pltpu.VMEM((GROUP, 8, TILE), F32),
            pltpu.VMEM((GROUP, 8, TILE), F32),
            pltpu.SemaphoreType.DMA,
            pltpu.SemaphoreType.DMA,
            pltpu.SemaphoreType.DMA((2,)),
            pltpu.SemaphoreType.DMA,
            pltpu.SemaphoreType.DMA((2,)),
            pltpu.SemaphoreType.DMA((4,)),
        ],
        compiler_params=pltpu.CompilerParams(collective_id=0, has_side_effects=True),
        name="pdlp",
    )(
        tiles.reshape(SLOTS, TILE, TILE),
        tile_rows.reshape(SLOTS),
        tile_cols.reshape(SLOTS),
        tile_counts.reshape(1),
        blocked(objective),
        blocked(upper),
        blocked(bound_codes),
        blocked(rhs),
        blocked(row_codes),
    )
    return primal.reshape(-1), dual.reshape(-1)


def solution(mesh):
    placed = (
        P("row", "col", None, None, None),
        P("row", "col", None),
        P("row", "col", None),
        P("row", "col"),
        P("col"),
        P("col"),
        P("col"),
        P("row"),
        P("row"),
    )
    return jax.shard_map(
        per_device, mesh=mesh, in_specs=placed, out_specs=(P("col"), P("row")), check_vma=False
    )
```

```python
import jax
import jax.numpy as jnp
from jax import lax
from jax.experimental import pallas as pl
from jax.experimental.pallas import tpu as pltpu
from jax.sharding import PartitionSpec as P

MESH = pl.DeviceIdType.MESH
TILE = 128
SLOTS = 16
GRID = 64
FULL = GRID + SLOTS
OUTER = 2
INNER = 4
STEPS = OUTER * INNER
GROUP = 16
CHIPS = 8
MSG = SLOTS + 1
ROOM = 24
BOTH = FULL + 1
PAIRS = SLOTS // 2
START = 3
F32 = jnp.float32
BF16 = jnp.bfloat16


def split3(x):
    hi = x.astype(BF16)
    rest = x - hi.astype(F32)
    mid = rest.astype(BF16)
    lo = (rest - mid.astype(F32)).astype(BF16)
    return hi, mid, lo


def total(x):
    return jnp.sum(jnp.sum(x, axis=0, keepdims=True), axis=1, keepdims=True)


def col_peers(row, col):
    x, y = col // 4, col % 4
    offsets = [(dx, dy) for dx in range(4) for dy in range(4) if dx or dy]
    offsets.sort(key=lambda o: -(min(o[0], 4 - o[0]) + min(o[1], 4 - o[1])))
    return [(row, ((x + dx) % 4) * 4 + (y + dy) % 4) for dx, dy in offsets]


def row_peers(row, col, cores):
    z, core = row // 2, row % 2
    offsets = [(dz, dc) for dz in range(CHIPS) for dc in range(cores) if dz or dc]
    offsets.sort(key=lambda o: -(min(o[0], CHIPS - o[0]) * 2 + o[1]))
    return [(((z + dz) % CHIPS) * 2 + (core + dc) % 2, col) for dz, dc in offsets]


def kernel(
    tiles_hbm, slot_rows_hbm, slot_cols_hbm, counts_hbm, objective_hbm, upper_hbm, bound_hbm, rhs_hbm, codes_hbm,
    primal_out, dual_out,
    tiles, slot_rows, slot_cols, counts, objective, upper, bound_codes, rhs, row_codes,
    w_forward, w_backward, sum_forward, sum_backward,
    obj, lower, higher, right, floor,
    s_primal, s_dual, s_rows, s_cols, t_primal, t_dual, t_rows, t_cols, b_primal, b_dual,
    scalars, col_buf, row_buf, core_out, core_in, col_start, row_start, my_slots, its_slots,
    fetch_sem, col_send, col_recv, row_send, row_recv, core_send, core_recv, start_sem,
):
    row, col = lax.axis_index("row"), lax.axis_index("col")
    chip, core = row // 2, row % 2
    by_col, by_row = col_peers(row, col), row_peers(row, col, 2)
    by_chip = row_peers(row, col, 1)
    sibling = (chip * 2 + (core + 1) % 2, col)
    barrier = pltpu.get_barrier_semaphore()
    for peer in by_col + by_row:
        pl.semaphore_signal(barrier, inc=1, device_id=peer, device_id_type=MESH)
    fetches = [
        pltpu.make_async_copy(src, dst, fetch_sem.at[i])
        for i, (src, dst) in enumerate((
            (counts_hbm, counts), (slot_rows_hbm, slot_rows), (slot_cols_hbm, slot_cols), (tiles_hbm, tiles),
            (rhs_hbm, rhs), (objective_hbm, objective), (upper_hbm, upper), (bound_hbm, bound_codes),
            (codes_hbm, row_codes),
        ))
    ]
    for fetch in fetches:
        fetch.start()

    def send_to(src, dst, peer, send, recv):
        pltpu.make_async_remote_copy(
            src_ref=src, dst_ref=dst, send_sem=send, recv_sem=recv,
            device_id=peer, device_id_type=MESH,
        ).start()

    def exchange(slots, me, rows, peers, send, recv):
        mine = slots.at[me, 0:rows]
        for peer in peers:
            send_to(mine, mine, peer, send, recv)

    def wait_for(shape, sem):
        pltpu.make_async_copy(shape, shape, sem).wait()

    def arrive(slots, rows, number, send, recv):
        others = slots.at[pl.ds(0, number), 0:rows]
        wait_for(others, recv)
        wait_for(others, send)

    ones = jnp.ones((1, TILE), F32)
    lane = lax.broadcasted_iota(jnp.int32, (1, TILE), 1)
    for state in (s_primal, s_dual, s_rows, s_cols, t_primal, t_dual, t_rows, t_cols, b_primal, b_dual):
        state[...] = jnp.zeros_like(state)
    for fetch in fetches:
        fetch.wait()

    live = counts[0]
    largest = jnp.zeros((8, TILE), F32)
    for t in range(SLOTS):
        size = jnp.max(jnp.abs(tiles[t]).reshape(16, 8, TILE), axis=0)
        largest = jnp.where(t < live, jnp.maximum(largest, size), largest)

    def index_row(indices, first):
        placed = jnp.zeros((1, TILE), F32)
        for t in range(SLOTS):
            placed = jnp.where(lane == first + t, indices[t].astype(F32), placed)
        return placed

    def slot_column(indices):
        which = lax.broadcasted_iota(jnp.int32, (SLOTS, TILE), 0)
        column = jnp.zeros((SLOTS, TILE), F32)
        for t in range(SLOTS):
            column = jnp.where(which == t, indices[t].astype(F32), column)
        return column

    row_start[row, 0:1, :] = index_row(slot_cols, chip * SLOTS)
    row_start[row, 1:2, :] = jnp.where(
        lane == 0,
        jnp.max(jnp.max(largest, axis=0, keepdims=True), axis=1, keepdims=True),
        total(rhs[...] * rhs[...]),
    )
    my_slots[...] = slot_column(slot_cols)
    pl.semaphore_wait(barrier, 2 * (GROUP - 1))
    exchange(row_start, row, 2, by_row, start_sem.at[0], start_sem.at[1])
    send_to(my_slots, its_slots, sibling, start_sem.at[4], start_sem.at[5])

    for t in range(SLOTS):
        tile = jnp.where(t < live, tiles[t], 0.0)
        at = slice(TILE * (t % 2), TILE * (t % 2) + TILE)
        for weights, block in ((w_backward, tile), (w_forward, tile.T)):
            hi = block.astype(BF16)
            weights[t // 2, 0:TILE, at] = hi
            weights[t // 2, TILE : 2 * TILE, at] = (block - hi.astype(F32)).astype(BF16)

    infinity = jnp.inf
    obj[0:GRID, :] = objective[...]
    right[0:GRID, :] = rhs[...]
    lower[0:GRID, :] = jnp.where(bound_codes[...] >= 1, 0.0, -infinity)
    higher[0:GRID, :] = jnp.where(bound_codes[...] == 2, upper[...], infinity)
    floor[0:GRID, :] = jnp.where(row_codes[...] == 1, 0.0, -infinity)
    for t in range(SLOTS):
        at = slice(GRID + t, GRID + t + 1)
        i, j = pl.ds(slot_rows[t], 1), pl.ds(slot_cols[t], 1)
        obj[at, :] = objective[j, :]
        right[at, :] = rhs[i, :]
        lower[at, :] = jnp.where(bound_codes[j, :] >= 1, 0.0, -infinity)
        higher[at, :] = jnp.where(bound_codes[j, :] == 2, upper[j, :], infinity)
        floor[at, :] = jnp.where(row_codes[i, :] == 1, 0.0, -infinity)

    half = col // CHIPS
    at_rows = index_row(slot_rows, (col % CHIPS) * SLOTS)
    col_start[col, 0:1, :] = jnp.where(half == 0, at_rows, 0.0)
    col_start[col, 1:2, :] = jnp.where(half == 1, at_rows, 0.0)
    object_part = total(objective[...] * objective[...])

    arrive(row_start, 2, GROUP - 1, start_sem.at[0], start_sem.at[1])
    parts = row_start[:, 1, :]
    most = jnp.max(parts, axis=0, keepdims=True)[:, 0:1]
    right_sq = jnp.sum(parts, axis=0, keepdims=True)[:, 1:2]
    col_start[col, 2:3, :] = jnp.where(lane == 0, most, object_part)
    exchange(col_start, col, START, by_col, start_sem.at[2], start_sem.at[3])

    def one_hot(wanted, entries):
        return jnp.where(wanted == entries, 1.0, 0.0).astype(BF16)

    wait_for(its_slots, start_sem.at[5])
    wait_for(my_slots, start_sem.at[4])
    block = lax.broadcasted_iota(jnp.int32, (GRID, TILE), 0).astype(F32)
    entries = sum(
        jnp.where(core == n % 2, row_start[n, 0:1, :], 0.0) for n in range(GROUP)
    )
    sum_backward[0:GRID, :] = one_hot(block, entries)
    sum_backward[GRID:FULL, :] = one_hot(my_slots[...], entries)
    sum_backward[FULL : FULL + SLOTS, :] = one_hot(its_slots[...], entries)
    at_slots = slot_column(slot_rows)

    arrive(col_start, START, GROUP - 1, start_sem.at[2], start_sem.at[3])
    parts = col_start[:, 2, :]
    most = jnp.max(parts, axis=0, keepdims=True)[:, 0:1]
    object_sq = jnp.sum(parts, axis=0, keepdims=True)[:, 1:2]
    scalars[0:1, :] = 0.05 / (most + 1e-06) * ones
    scalars[1:2, :] = jnp.sqrt((object_sq + 1e-06) / (right_sq + 1e-06)) * ones
    scalars[2:3, :] = jnp.zeros((1, TILE), F32)
    for n in range(2):
        entries = jnp.sum(col_start[:, n, :], axis=0, keepdims=True)
        at = slice(n * TILE, n * TILE + TILE)
        sum_forward[0:GRID, at] = one_hot(block, entries)
        sum_forward[GRID:FULL, at] = one_hot(at_slots, entries)

    def images(weights, pieces):
        stacked = jnp.concatenate(split3(pieces), axis=0)
        operand = jnp.concatenate([stacked, stacked], axis=1)
        which = lax.broadcasted_iota(jnp.int32, (8, TILE), 0)
        halves = [jnp.zeros((8, TILE), F32), jnp.zeros((8, TILE), F32)]
        for pair in range(PAIRS):
            product = jnp.dot(operand, weights[pair], preferred_element_type=F32)
            side, first = pair // 4, 2 * pair % 8
            base = 8 * side
            both = sum(product[base + SLOTS * s : base + SLOTS * s + 8, :] for s in range(3))
            halves[side] = jnp.where(which == first, both[:, 0:TILE], halves[side])
            halves[side] = jnp.where(which == first + 1, both[:, TILE : 2 * TILE], halves[side])
        return halves

    def summed_rows(matrix, slots):
        data = slots[:, 0:SLOTS, :].reshape(-1, TILE)
        ones_at = matrix[...]
        return sum(jnp.dot(ones_at, part, preferred_element_type=F32) for part in split3(data))

    def post(slots, me, halves, sums):
        slots[me, 0:8, :] = halves[0]
        slots[me, 8:SLOTS, :] = halves[1]
        lanes = jnp.zeros((1, TILE), F32)
        for i, value in enumerate(sums):
            lanes = jnp.where(lane == i, value, lanes)
        slots[me, SLOTS:MSG, :] = lanes

    def gathered_sums(slots):
        return jnp.sum(slots[:, SLOTS, :], axis=0, keepdims=True)

    def iteration(k, _):
        parity = lax.rem(k, 2)
        last = k == STEPS - 1
        restart = k == INNER - 1
        step, weight = scalars[0:1, :], scalars[1:2, :]
        weight_total = scalars[2:3, :] + step
        primal = s_primal[...]
        next_primal = jnp.minimum(
            jnp.maximum(primal - step / weight * (obj[...] - s_cols[...]), lower[...]), higher[...]
        )
        halves = images(w_forward, next_primal[GRID:FULL, :])
        total_primal = t_primal[...] + step * next_primal
        mean_primal = total_primal / weight_total
        move = (next_primal - primal)[0:GRID, :]
        drift = (mean_primal - b_primal[...])[0:GRID, :]
        slots = col_buf.at[parity]
        post(slots, col, halves, (total(move * move), total(drift * drift)))
        exchange(slots, col, MSG, by_col, col_send, col_recv.at[parity])
        s_primal[...] = jnp.where(restart, mean_primal, next_primal)
        t_primal[...] = jnp.where(restart, 0.0, total_primal)
        b_primal[...] = jnp.where(restart, mean_primal, b_primal[...])

        @pl.when(last)
        def _():
            primal_out[...] = mean_primal[0:GRID, :]

        arrive(slots, MSG, GROUP - 1, col_send, col_recv.at[parity])
        next_rows = summed_rows(sum_forward, slots)
        sums = gathered_sums(slots)
        primal_sq, primal_drift = sums[:, 0:1], sums[:, 1:2]
        rows = s_rows[...]
        dual = s_dual[...]
        next_dual = jnp.maximum(
            dual + step * weight * (right[...] - (2.0 * next_rows - rows)), floor[...]
        )
        total_dual = t_dual[...] + step * next_dual
        mean_dual = total_dual / weight_total

        @pl.when(last)
        def _():
            dual_out[...] = mean_dual[0:GRID, :]

        @pl.when(jnp.logical_not(last))
        def _():
            halves = images(w_backward, next_dual[GRID:FULL, :])
            move = (next_dual - dual)[0:GRID, :]
            image_move = (next_rows - rows)[0:GRID, :]
            drift = (mean_dual - b_dual[...])[0:GRID, :]
            slots = row_buf.at[parity]
            post(slots, chip, halves, (total(move * move), total(move * image_move), total(drift * drift)))
            exchange(slots, chip, MSG, by_chip, row_send, row_recv.at[parity])
            total_rows = t_rows[...] + step * next_rows
            s_dual[...] = jnp.where(restart, mean_dual, next_dual)
            t_dual[...] = jnp.where(restart, 0.0, total_dual)
            b_dual[...] = jnp.where(restart, mean_dual, b_dual[...])
            s_rows[...] = jnp.where(restart, total_rows / weight_total, next_rows)
            t_rows[...] = jnp.where(restart, 0.0, total_rows)

            shrink, growth = jnp.float32(0.0), jnp.float32(0.0)
            for i in range(STEPS - 1):
                shrink = jnp.where(k == i, jnp.float32(1.0 - (i + 2) ** (-0.3)), shrink)
                growth = jnp.where(k == i, jnp.float32(1.0 + (i + 2) ** (-0.6)), growth)

            arrive(slots, MSG, CHIPS - 1, row_send, row_recv.at[parity])
            mine = summed_rows(sum_backward, slots)
            sums = gathered_sums(slots)
            core_out[0:GRID, :] = mine[0:GRID, :]
            core_out[GRID:FULL, :] = mine[FULL : FULL + SLOTS, :]
            core_out[FULL:BOTH, :] = sums
            outgoing, incoming = core_out.at[0:BOTH], core_in.at[parity, 0:BOTH]
            send_to(outgoing, incoming, sibling, core_send, core_recv.at[parity])
            wait_for(incoming, core_recv.at[parity])
            wait_for(outgoing, core_send)
            next_cols = mine[0:FULL, :] + core_in[parity, 0:FULL, :]
            sums = sums + core_in[parity, FULL:BOTH, :]
            dual_sq, inter, dual_drift = sums[:, 0:1], sums[:, 1:2], sums[:, 2:3]
            numer = shrink * (weight * primal_sq + dual_sq / weight + 1e-06)
            new_step = numer / jnp.maximum(2.0 * jnp.abs(inter), numer / (growth * step))
            new_weight = jnp.sqrt(
                weight * jnp.sqrt(dual_drift + 1e-06) / jnp.sqrt(primal_drift + 1e-06)
            )
            total_cols = t_cols[...] + step * next_cols
            s_cols[...] = jnp.where(restart, total_cols / weight_total, next_cols)
            t_cols[...] = jnp.where(restart, 0.0, total_cols)
            scalars[0:1, :] = new_step
            scalars[1:2, :] = jnp.where(restart, new_weight, weight)
            scalars[2:3, :] = jnp.where(restart, 0.0, weight_total)

        return 0

    lax.fori_loop(0, STEPS, iteration, 0)


def per_device(
    tiles, tile_rows, tile_cols, tile_counts, objective, upper, bound_codes, rhs, row_codes
):
    blocked = lambda v: v.reshape(GRID, TILE)
    block = lambda dtype: pltpu.VMEM((GRID, TILE), dtype)
    anywhere = pl.BlockSpec(memory_space=pl.ANY)
    vmem = pl.BlockSpec(memory_space=pltpu.VMEM)
    dma = pltpu.SemaphoreType.DMA
    primal, dual = pl.pallas_call(
        kernel,
        out_shape=(jax.ShapeDtypeStruct((GRID, TILE), F32),) * 2,
        in_specs=[anywhere] * 9,
        out_specs=(vmem, vmem),
        scratch_shapes=[
            pltpu.VMEM((SLOTS, TILE, TILE), F32),
            pltpu.SMEM((SLOTS,), jnp.int32),
            pltpu.SMEM((SLOTS,), jnp.int32),
            pltpu.SMEM((1,), jnp.int32),
            block(F32), block(F32), block(jnp.int32), block(F32), block(jnp.int32),
            pltpu.VMEM((PAIRS, 2 * TILE, 2 * TILE), BF16),
            pltpu.VMEM((PAIRS, 2 * TILE, 2 * TILE), BF16),
            pltpu.VMEM((FULL, 2 * TILE), BF16),
            pltpu.VMEM((FULL + SLOTS, TILE), BF16),
        ]
        + [pltpu.VMEM((FULL, TILE), F32) for _ in range(15)]
        + [
            pltpu.VMEM((8, TILE), F32),
            pltpu.VMEM((2, GROUP, ROOM, TILE), F32),
            pltpu.VMEM((2, CHIPS, ROOM, TILE), F32),
            pltpu.VMEM((FULL + 8, TILE), F32),
            pltpu.VMEM((2, FULL + 8, TILE), F32),
            pltpu.VMEM((GROUP, 8, TILE), F32),
            pltpu.VMEM((GROUP, 8, TILE), F32),
            pltpu.VMEM((SLOTS, TILE), F32),
            pltpu.VMEM((SLOTS, TILE), F32),
            dma((9,)), dma, dma((2,)), dma, dma((2,)), dma, dma((2,)), dma((6,)),
        ],
        compiler_params=pltpu.CompilerParams(collective_id=0, has_side_effects=True),
        name="pdlp",
    )(
        tiles.reshape(SLOTS, TILE, TILE),
        tile_rows.reshape(SLOTS),
        tile_cols.reshape(SLOTS),
        tile_counts.reshape(1),
        blocked(objective),
        blocked(upper),
        blocked(bound_codes),
        blocked(rhs),
        blocked(row_codes),
    )
    return primal.reshape(-1), dual.reshape(-1)


def solution(mesh):
    placed = (
        P("row", "col", None, None, None),
        P("row", "col", None),
        P("row", "col", None),
        P("row", "col"),
        P("col"),
        P("col"),
        P("col"),
        P("row"),
        P("row"),
    )
    return jax.shard_map(
        per_device, mesh=mesh, in_specs=placed, out_specs=(P("col"), P("row")), check_vma=False
    )
```
